32 devices in a mesh: bra: 4 (over z), ket: 2 (over y), pair: 4 (over x, core).
Axes of the slice: x: 2, y: 2, z: 4, core: 2. Of those that a mesh axis runs over, the one named last changes fastest.
Arguments:
- amplitudes: bfloat16 [1536, 8, 1536], P('pair', ('bra', 'ket')), may hold values from -6 to 6
- integrals: bfloat16 [8, 4, 128, 1536], P(('bra', 'ket'), 'pair'), may hold values from -0.25 to 0.25
- screen_list: int32 [8, 4], P(('bra', 'ket')), may hold values from 0 to 11
- block_owner: int32 [8, 4], P(('bra', 'ket')), may hold values from 0 to 7, all different within a row
- mirror_map: int32 [8, 1536], replicated, may hold values from 0 to 1535, as said below
- pair_virt: int32 [8, 2, 1536], P(('bra', 'ket')), may hold values from 0 to 2047, as said below
- vir_energy: float32 [2048], replicated, may hold values from 0.1 to 1.5
- pair_energy: float32 [1536], P('pair'), may hold values from -1.5 to -0.4
Outputs:
- new_amplitudes: bfloat16 [1536, 8, 1536], P('pair', ('bra', 'ket'))
The draws below stay inside these ranges and needn't reach their ends.
Inputs may be any that keep to these rules, and one draw needn't show every extreme that they name: `block_owner`: the 4 entries of a row are distinct. `mirror_map`: every row is a permutation of 0 to 1535, and row t + 4 is the inverse permutation of row t. `pair_virt`: if position p of tile t < 4 holds the orbitals (a, b), position mirror_map[t, p] of tile t + 4 holds (b, a).
All inputs are finite; a program needn't handle non-finite values.
Results may differ from the reference program's by a relative error of at most 0.0045.
Values may be sent and summed in bfloat16 or wider, within the bound.
A program may use at most 64 MiB of HBM per device.

```python
import math
import jax
import jax.numpy as jnp
from jax import lax

NV = 2048
BLK = 1536
SEG = 128
OCC = 1536
TILES = 8
NBLK = 4
SEGS = 12


def mirror_helper(key):
    half_tiles = TILES // 2
    keys = jax.random.split(jax.random.fold_in(key, 7), half_tiles)
    forward = jax.vmap(lambda single: jax.random.permutation(single, BLK))(keys).astype(jnp.int32)

    def invert(perm):
        return jnp.zeros((BLK,), jnp.int32).at[perm].set(jnp.arange(BLK, dtype=jnp.int32))
    inverse = jax.vmap(invert)(forward)
    return (forward, inverse)


def draw_mirror_map(key, part):
    forward, inverse = mirror_helper(key)
    return jnp.concatenate([forward, inverse], 0)


def draw_pair_virt(key, part):
    half_tiles = TILES // 2
    forward, inverse = mirror_helper(key)
    first = jax.random.randint(jax.random.fold_in(key, 11), (half_tiles, BLK), 0, NV).astype(jnp.int32)
    second = jax.random.randint(jax.random.fold_in(key, 13), (half_tiles, BLK), 0, NV).astype(jnp.int32)
    first = first.at[0, 0].set(0).at[0, 1].set(NV - 1)
    lower_pairs = jnp.stack([first, second], 1)
    upper_first = jnp.take_along_axis(second, inverse, axis=1)
    upper_second = jnp.take_along_axis(first, inverse, axis=1)
    upper_pairs = jnp.stack([upper_first, upper_second], 1)
    return jnp.concatenate([lower_pairs, upper_pairs], 0)


def place_ends(entries, key, smallest, largest):
    place = [jax.random.randint(jax.random.fold_in(key, axis), (), 0, length) for axis, length in enumerate(entries.shape)]
    longest = entries.shape.index(max(entries.shape))
    neighbour = place[:longest] + [(place[longest] + 1) % entries.shape[longest]] + place[longest + 1:]
    return entries.at[tuple(place)].set(smallest).at[tuple(neighbour)].set(largest)


def shard_levels(own_key, shape, cuts, smallest, top_value):
    gain, own = 1.0, jax.random.fold_in(own_key, 6)
    for axis_at, shards_of in cuts:
        steps = jnp.exp(jax.random.uniform(jax.random.fold_in(own, axis_at), (shards_of,), jnp.float32, smallest / len(cuts), top_value / len(cuts)))
        gain = gain * jnp.repeat(steps, shape[axis_at] // shards_of).reshape([-1 if axis == axis_at else 1 for axis in range(len(shape))])
    return gain


def distinct(own_key, rows, number_of, top, lift):
    order = jax.random.permutation(jax.random.fold_in(own_key, 1), number_of)
    boost = order
    for power in range(3):
        boost = boost * boost // number_of
    boost = boost * lift // number_of
    tickets = jax.random.randint(jax.random.fold_in(own_key, 2), (rows, number_of), 0, 4096) + boost
    holders = jax.random.permutation(jax.random.fold_in(own_key, 3), rows)[jnp.arange(number_of) % rows]
    tickets = jnp.where(jnp.arange(rows)[:, None] == holders[None, :], 1 << 14, tickets)
    score = tickets * number_of + jnp.arange(number_of)
    return lax.top_k(score.astype(jnp.int32), top)[1].astype(jnp.int32)


def normal_values(rng, dims, deviation, limit, cuts=(), kind=jnp.bfloat16):
    result = deviation * jax.random.normal(rng, dims, jnp.float32)
    if cuts:
        result = result * shard_levels(rng, dims, cuts, -0.22, 0.18)
    return jnp.clip(result, -limit, limit).astype(kind)


def setup_inputs(seed: int = 0) -> dict:
    key_list = jax.random.split(jax.random.key(seed), 9)
    amplitudes = normal_values(key_list[0], (OCC, TILES, BLK), 1.0, 6.0, ((0, 4), (1, 8)))
    integrals = normal_values(key_list[1], (TILES, NBLK, SEG, BLK), (NBLK * SEG) ** -0.5, 0.25, ((0, 8), (1, 4)))
    screen_list = place_ends(jax.random.randint(key_list[2], (TILES, NBLK), 0, SEGS), jax.random.fold_in(key_list[2], 1), 0, SEGS - 1).astype(jnp.int32)
    block_owner = distinct(key_list[3], TILES, TILES, NBLK, 8192)
    mirror_map = draw_mirror_map(jax.random.fold_in(key_list[8], 71), 0)
    pair_virt = draw_pair_virt(jax.random.fold_in(key_list[8], 71), 0)
    vir_energy = jnp.clip(jnp.exp(jax.random.uniform(key_list[6], (NV,), jnp.float32, math.log(0.1), math.log(1.5))), 0.1, 1.5)
    pair_energy = jnp.clip(-1.5 + 1.1 * jax.random.uniform(key_list[7], (OCC,), jnp.float32) ** shard_levels(key_list[7], (OCC,), ((0, 4),), -0.2, 0.2), -1.5, -0.4)
    return {"amplitudes": amplitudes, "integrals": integrals, "screen_list": screen_list, "block_owner": block_owner, "mirror_map": mirror_map, "pair_virt": pair_virt, "vir_energy": vir_energy, "pair_energy": pair_energy}


def permute_columns(tile_data, indices):
    return jnp.take(tile_data, indices, axis=1)


def reference(amplitudes, integrals, screen_list, block_owner, mirror_map, pair_virt, vir_energy, pair_energy):
    occupied, tile_count, block_len = amplitudes.shape
    half_tiles = tile_count // 2
    seg_width = integrals.shape[2]
    seg_count = block_len // seg_width
    permute_tiles = jax.vmap(permute_columns, in_axes=(1, 0), out_axes=1)
    permute_rows = jax.vmap(permute_columns, in_axes=(0, 0), out_axes=0)
    lower_raw = amplitudes[:, :half_tiles, :]
    upper_raw = amplitudes[:, half_tiles:, :]
    map_lower = mirror_map[:half_tiles]
    map_upper = mirror_map[half_tiles:]
    sym_fold = ((lower_raw.astype(jnp.float32) + permute_tiles(upper_raw, map_lower).astype(jnp.float32)) * 0.5).astype(jnp.bfloat16)
    anti_fold = ((upper_raw.astype(jnp.float32) - permute_tiles(lower_raw, map_upper).astype(jnp.float32)) * 0.5).astype(jnp.bfloat16)
    sym_segments = sym_fold.reshape(occupied, half_tiles, seg_count, seg_width)
    anti_segments = anti_fold.reshape(occupied, half_tiles, seg_count, seg_width)

    def one_tile(packed):
        tile_id, owners_row, segments_row, blocks = packed
        source = owners_row % half_tiles
        from_sym = sym_segments[:, source, segments_row, :]
        from_anti = anti_segments[:, source, segments_row, :]
        operand = jnp.where(tile_id >= half_tiles, from_anti, from_sym)
        return jnp.dot(operand.reshape(occupied, -1), blocks.reshape(-1, block_len), preferred_element_type=jnp.float32)

    ladder = lax.map(one_tile, (jnp.arange(tile_count, dtype=jnp.int32), block_owner, screen_list, integrals))
    resid_lower = ladder[:half_tiles] - permute_rows(ladder[half_tiles:], map_lower)
    resid_upper = ladder[half_tiles:] + permute_rows(ladder[:half_tiles], map_upper)
    residual = jnp.transpose(jnp.concatenate([resid_lower, resid_upper], 0), (1, 0, 2))
    energy_first = jnp.take(vir_energy, pair_virt[:, 0, :])
    energy_second = jnp.take(vir_energy, pair_virt[:, 1, :])
    denominator = pair_energy[:, None, None] - energy_first[None] - energy_second[None]
    return (amplitudes.astype(jnp.float32) + residual / denominator).astype(jnp.bfloat16)
```

```python
import functools

import jax
import jax.numpy as jnp
from jax import lax
from jax.experimental import pallas as pl
from jax.experimental.pallas import tpu as pltpu
from jax.sharding import PartitionSpec as P

OWNERS = ("bra", "ket")
VMEM = pltpu.VMEM
SMEM = pltpu.SMEM


def swap(block, axis, bit):
    count = lax.axis_size(axis)
    return lax.ppermute(block, axis, [(i, i ^ bit) for i in range(count)])


def column_step(length):
    return next(step for step in (512, 256, 128, length) if length % step == 0)


def params(limit=48 << 20):
    return pltpu.CompilerParams(vmem_limit_bytes=limit)


def select_kernel(seg_width, segs_ref, tile_ref, col_a_ref, col_b_ref, out_ref):
    dest = pl.program_id(0)
    length = tile_ref.shape[1]
    lane = lax.broadcasted_iota(jnp.int32, (length, seg_width), 1)
    hots = []
    for sub in range(4):
        col = (col_a_ref, col_b_ref)[sub // 2]
        base = segs_ref[dest * 4 + sub] * seg_width
        hots.append((col[...] == lane + base).astype(jnp.float32).astype(jnp.bfloat16))
    hot = jnp.concatenate(hots, axis=1)
    out_ref[0] = jnp.dot(tile_ref[...], hot, preferred_element_type=jnp.float32).astype(
        jnp.bfloat16
    )


def select_segments(tile, col_a, col_b, segs, seg_width):
    rows, length = tile.shape
    dests = segs.shape[0] // 4
    return pl.pallas_call(
        functools.partial(select_kernel, seg_width),
        grid=(dests,),
        in_specs=[
            pl.BlockSpec(memory_space=SMEM),
            pl.BlockSpec((rows, length), lambda d: (0, 0)),
            pl.BlockSpec((length, 1), lambda d: (0, 0)),
            pl.BlockSpec((length, 1), lambda d: (0, 0)),
        ],
        out_specs=pl.BlockSpec((1, rows, 4 * seg_width), lambda d: (d, 0, 0)),
        out_shape=jax.ShapeDtypeStruct((dests, rows, 4 * seg_width), jnp.bfloat16),
        compiler_params=params(),
        cost_estimate=pl.CostEstimate(
            flops=2 * rows * length * 4 * seg_width * dests,
            bytes_accessed=2 * rows * (length + dests * 4 * seg_width),
            transcendentals=0,
        ),
    )(segs, tile, col_a, col_b)


def permute_kernel(sign_ref, block_ref, col_ref, out_ref):
    step = out_ref.shape[1]
    length = block_ref.shape[1]
    lane = lax.broadcasted_iota(jnp.int32, (length, step), 1) + pl.program_id(0) * step
    hot = (col_ref[...] == lane).astype(jnp.float32).astype(jnp.bfloat16)
    moved = jnp.dot(block_ref[...], hot, preferred_element_type=jnp.float32)
    out_ref[...] = (moved * sign_ref[0]).astype(jnp.bfloat16)


def permute_block(block, col, sign):
    rows, length = block.shape
    step = column_step(length)
    return pl.pallas_call(
        permute_kernel,
        grid=(length // step,),
        in_specs=[
            pl.BlockSpec(memory_space=SMEM),
            pl.BlockSpec((rows, length), lambda j: (0, 0)),
            pl.BlockSpec((length, 1), lambda j: (0, 0)),
        ],
        out_specs=pl.BlockSpec((rows, step), lambda j: (0, j)),
        out_shape=jax.ShapeDtypeStruct((rows, length), jnp.bfloat16),
        compiler_params=params(),
        cost_estimate=pl.CostEstimate(
            flops=2 * rows * length * length, bytes_accessed=4 * rows * length, transcendentals=0
        ),
    )(sign, block, col)


def energy_kernel(table_ref, index_ref, out_ref):
    count = table_ref.shape[1]
    step = out_ref.shape[1]
    value = table_ref[...]
    high = value.astype(jnp.bfloat16)
    rest = value - high.astype(jnp.float32)
    middle = rest.astype(jnp.bfloat16)
    low = (rest - middle.astype(jnp.float32)).astype(jnp.bfloat16)
    spot = lax.broadcasted_iota(jnp.int32, (count, step), 0)
    for row in range(2):
        hot = (spot == index_ref[row : row + 1, :]).astype(jnp.float32).astype(jnp.bfloat16)
        parts = [
            jnp.dot(piece, hot, preferred_element_type=jnp.float32)
            for piece in (high, middle, low)
        ]
        out_ref[row : row + 1, :] = (parts[0][0:1] + parts[1][0:1]) + parts[2][0:1]


def pair_energies(vir_energy, index):
    count = vir_energy.shape[0]
    length = index.shape[1]
    step = column_step(length)
    table = jnp.broadcast_to(vir_energy[None, :], (8, count))
    return pl.pallas_call(
        energy_kernel,
        grid=(length // step,),
        in_specs=[
            pl.BlockSpec((8, count), lambda j: (0, 0)),
            pl.BlockSpec((2, step), lambda j: (0, j)),
        ],
        out_specs=pl.BlockSpec((2, step), lambda j: (0, j)),
        out_shape=jax.ShapeDtypeStruct((2, length), jnp.float32),
        compiler_params=params(),
        cost_estimate=pl.CostEstimate(
            flops=2 * 256 * count * length * 2, bytes_accessed=4 * count * 8, transcendentals=0
        ),
    )(table, index)


def assemble_kernel(source_ref, sub_ref, in_ref, out_ref):
    out_ref[...] = in_ref[0]


def assemble(messages, source, sub, seg_width):
    rows = messages.shape[1]
    slots = source.shape[0]
    return pl.pallas_call(
        assemble_kernel,
        grid_spec=pltpu.PrefetchScalarGridSpec(
            num_scalar_prefetch=2,
            grid=(slots,),
            in_specs=[
                pl.BlockSpec((1, rows, seg_width), lambda j, src, sub: (src[j], 0, sub[j]))
            ],
            out_specs=pl.BlockSpec((rows, seg_width), lambda j, src, sub: (0, j)),
        ),
        out_shape=jax.ShapeDtypeStruct((rows, slots * seg_width), jnp.bfloat16),
        compiler_params=params(),
        cost_estimate=pl.CostEstimate(
            flops=0, bytes_accessed=4 * rows * slots * seg_width, transcendentals=0
        ),
    )(source, sub, messages)


def final_kernel(
    pieces, flag_ref, mine_ref, recv_ref, tile_ref, pair_ref, vir_ref, *rest
):
    blocks = rest[: 2 * pieces]
    out_ref, own_ref, other_ref = rest[2 * pieces :]
    width = own_ref.shape[1]

    @pl.when(pl.program_id(0) == 0)
    def _():
        upper = flag_ref[0] > 0
        mine_a = mine_ref[:, :width].astype(jnp.float32)
        recv_a = recv_ref[:, :width].astype(jnp.float32)
        mine_b = mine_ref[:, width:].astype(jnp.float32)
        recv_b = recv_ref[:, width:].astype(jnp.float32)
        sym = ((mine_a + recv_a) * 0.5).astype(jnp.bfloat16)
        sign = jnp.where(upper, 0.5, -0.5).astype(jnp.float32)
        anti = ((mine_b - recv_b) * sign).astype(jnp.bfloat16)

        @pl.when(upper)
        def _():
            own_ref[...] = anti
            other_ref[...] = sym

        @pl.when(jnp.logical_not(upper))
        def _():
            own_ref[...] = sym
            other_ref[...] = anti

    depth = blocks[0].shape[0]
    total = None
    for held, part in ((own_ref, blocks[:pieces]), (other_ref, blocks[pieces:])):
        for at, block in enumerate(part):
            term = jnp.dot(
                held[:, at * depth : (at + 1) * depth],
                block[...],
                preferred_element_type=jnp.float32,
            )
            total = term if total is None else total + term
    denominator = pair_ref[...] - vir_ref[0:1, :] - vir_ref[1:2, :]
    out_ref[...] = (tile_ref[...].astype(jnp.float32) + total / denominator).astype(jnp.bfloat16)


def finish(flag, mine, recv, tile, pair_energy, energies, own_blocks, mirror_blocks):
    rows, length = tile.shape
    width = mine.shape[1] // 2
    step = 256 if length % 256 == 0 else column_step(length)
    pieces = len(own_blocks)
    depth = own_blocks[0].shape[0]
    whole = lambda j: (0, 0)
    across = lambda j: (0, j)
    return pl.pallas_call(
        functools.partial(final_kernel, pieces),
        grid=(length // step,),
        in_specs=[
            pl.BlockSpec(memory_space=SMEM),
            pl.BlockSpec(mine.shape, whole),
            pl.BlockSpec(recv.shape, whole),
            pl.BlockSpec((rows, step), across),
            pl.BlockSpec((rows, 1), whole),
            pl.BlockSpec((2, step), across),
        ]
        + [pl.BlockSpec((depth, step), across)] * (2 * pieces),
        out_specs=pl.BlockSpec((rows, step), across),
        out_shape=jax.ShapeDtypeStruct((rows, length), jnp.bfloat16),
        scratch_shapes=[VMEM((rows, width), jnp.bfloat16)] * 2,
        compiler_params=params(56 << 20),
        cost_estimate=pl.CostEstimate(
            flops=4 * rows * width * length,
            bytes_accessed=4 * (rows * length + width * length),
            transcendentals=0,
        ),
    )(flag, mine, recv, tile, pair_energy[:, None], energies, *own_blocks, *mirror_blocks)


def gather_pieces(block):
    pieces = [block]
    bit = lax.axis_size("pair") // 2
    order = [0]
    while bit:
        pieces += [swap(piece, "pair", bit) for piece in pieces]
        order += [at ^ bit for at in order]
        bit //= 2
    return pieces, order


def local(
    amplitudes, integrals, screen_list, block_owner, mirror_map, pair_virt, vir_energy, pair_energy
):
    owners = lax.axis_size(OWNERS)
    half = owners // 2
    self_index = lax.axis_index(OWNERS)
    upper = self_index >= half
    folded = self_index % half
    tile = amplitudes[:, 0, :]
    rows, length = tile.shape
    per, seg_width = integrals.shape[1:3]
    count = block_owner.shape[1]

    table = jnp.concatenate([block_owner, screen_list], axis=1)
    table = lax.all_to_all(
        jnp.broadcast_to(table, (owners, 2 * count)), OWNERS, split_axis=0, concat_axis=0, tiled=True
    )
    all_owner, all_screen = table[:, :count], table[:, count:]

    map_col = lax.dynamic_index_in_dim(mirror_map, self_index, 0, keepdims=False)[:, None]
    straight = lax.broadcasted_iota(jnp.int32, (length, 1), 0)
    col_a = jnp.where(upper, map_col, straight)
    col_b = jnp.where(upper, straight, map_col)
    shard = integrals[0].reshape(per * seg_width, length)
    sign = jnp.where(upper, -1.0, 1.0).astype(jnp.float32)[None]
    own_blocks, order = gather_pieces(shard)
    mirror_shard = swap(permute_block(shard, map_col, sign), OWNERS, half)
    mirror_blocks, _ = gather_pieces(mirror_shard)

    step = jnp.arange(half, dtype=jnp.int32)
    tiles = (folded ^ step)[:, None] + jnp.array([0, half], jnp.int32)[None, :]
    tile_hot = tiles[:, :, None] == jnp.arange(owners, dtype=jnp.int32)
    dest_owner = jnp.sum(jnp.where(tile_hot[..., None], all_owner, 0), axis=2)
    dest_screen = jnp.sum(jnp.where(tile_hot[..., None], all_screen, 0), axis=2)
    serving = folded + jnp.array([0, half], jnp.int32)
    match = dest_owner[:, :, None, :] == serving[None, None, :, None]
    segs = jnp.sum(jnp.where(match, dest_screen[:, :, None, :], 0), axis=3).reshape(-1)

    outgoing = select_segments(tile, col_a, col_b, segs, seg_width)
    messages = [outgoing[0]] + [swap(outgoing[d], OWNERS, d) for d in range(1, half)]

    pair_at = lax.axis_index("pair")
    slot = (
        jnp.concatenate([(pair_at ^ at) * per + jnp.arange(per, dtype=jnp.int32) for at in order])
    )
    slot_hot = slot[:, None] == jnp.arange(count, dtype=jnp.int32)[None, :]
    mine_owner = jnp.sum(jnp.where(slot_hot[None], dest_owner[0][:, None, :], 0), axis=2)
    source = ((mine_owner % half) ^ folded).reshape(-1)
    sub = (mine_owner // half + jnp.array([[0], [2]], jnp.int32)).reshape(-1)
    mine = assemble(jnp.stack(messages), source, sub, seg_width)
    recv = swap(mine, OWNERS, half)

    energies = pair_energies(vir_energy, pair_virt[0])
    flag = upper.astype(jnp.int32)[None]
    updated = finish(flag, mine, recv, tile, pair_energy, energies, own_blocks, mirror_blocks)
    return updated[:, None, :]


def solution(mesh):
    placed = (
        P("pair", OWNERS, None),
        P(OWNERS, "pair", None, None),
        P(OWNERS, None),
        P(OWNERS, None),
        P(),
        P(OWNERS, None, None),
        P(),
        P("pair"),
    )
    return jax.shard_map(
        local,
        mesh=mesh,
        in_specs=placed,
        out_specs=P("pair", OWNERS, None),
        check_vma=False,
    )
```

```python
import functools

import jax
import jax.numpy as jnp
from jax import lax
from jax.experimental import pallas as pl
from jax.experimental.pallas import tpu as pltpu
from jax.sharding import PartitionSpec as P

OWNERS = ("bra", "ket")
CHUNKS = 2
VMEM = pltpu.VMEM
SMEM = pltpu.SMEM


def swap(block, axis, bit):
    count = lax.axis_size(axis)
    return lax.ppermute(block, axis, [(i, i ^ bit) for i in range(count)])


def column_step(length):
    return next(step for step in (512, 256, 128, length) if length % step == 0)


def params(limit=48 << 20):
    return pltpu.CompilerParams(vmem_limit_bytes=limit)


def chunk_count(rows, half):
    if half > 8:
        return 1
    return next(c for c in (CHUNKS, 3, 2, 1) if c == 1 or rows % (16 * c) == 0)


def table_kernel(owners, ket, row_ref, out_ref, held, send_sem, recv_sem):
    me = lax.axis_index(OWNERS)
    peers = [me ^ d for d in range(owners)]
    places = [{"bra": peer // ket, "ket": peer % ket} for peer in peers]
    barrier = pltpu.get_barrier_semaphore()
    for d in range(1, owners):
        pl.semaphore_signal(
            barrier, inc=1, device_id=places[d], device_id_type=pl.DeviceIdType.MESH
        )
    pl.semaphore_wait(barrier, owners - 1)
    copies = []
    for d in range(1, owners):
        copy = pltpu.make_async_remote_copy(
            src_ref=row_ref,
            dst_ref=held.at[d],
            send_sem=send_sem.at[d],
            recv_sem=recv_sem.at[d],
            device_id=places[d],
            device_id_type=pl.DeviceIdType.MESH,
        )
        copy.start()
        copies.append(copy)
    out_ref[0:1, :] = row_ref[0:1, :]
    for d in range(1, owners):
        copies[d - 1].wait()
        out_ref[d : d + 1, :] = held[d, 0:1, :]


def exchange_tables(row):
    owners = lax.axis_size(OWNERS)
    width = row.shape[1]
    return pl.pallas_call(
        functools.partial(table_kernel, owners, lax.axis_size("ket")),
        in_specs=[pl.BlockSpec(memory_space=VMEM)],
        out_specs=pl.BlockSpec(memory_space=VMEM),
        out_shape=jax.ShapeDtypeStruct((owners, width), jnp.int32),
        scratch_shapes=[
            VMEM((owners, 8, width), jnp.int32),
            pltpu.SemaphoreType.DMA((owners,)),
            pltpu.SemaphoreType.DMA((owners,)),
        ],
        compiler_params=pltpu.CompilerParams(
            collective_id=1, has_side_effects=True, vmem_limit_bytes=8 << 20
        ),
    )(row)


def select_kernel(count, seg_width, segs_ref, tile_ref, col_a_ref, col_b_ref, *out_refs):
    dest = pl.program_id(0)
    half = pl.num_programs(0)
    flip = segs_ref[0, 2 * count] * half
    folded = segs_ref[0, 2 * count + 1]
    length = tile_ref.shape[1]
    lane = lax.broadcasted_iota(jnp.int32, (length, seg_width), 1)
    hots = []
    for sub in range(4):
        col = (col_a_ref, col_b_ref)[sub // 2]
        row = dest + (flip if sub < 2 else half - flip)
        serving = folded + (sub % 2) * half
        segment = jnp.int32(0)
        for k in range(count):
            held = segs_ref[row, k] == serving
            segment += jnp.where(held, segs_ref[row, count + k], 0)
        base = segment * seg_width
        hots.append((col[...] == lane + base).astype(jnp.float32).astype(jnp.bfloat16))
    hot = jnp.concatenate(hots, axis=1)
    part = out_refs[0].shape[1]
    for at, out_ref in enumerate(out_refs):
        out_ref[0] = jnp.dot(
            tile_ref[at * part : (at + 1) * part, :], hot, preferred_element_type=jnp.float32
        ).astype(jnp.bfloat16)


def select_segments(tile, col_a, col_b, segs, count, seg_width, chunks):
    rows, length = tile.shape
    dests = segs.shape[0] // 2
    return pl.pallas_call(
        functools.partial(select_kernel, count, seg_width),
        grid=(dests,),
        in_specs=[
            pl.BlockSpec(memory_space=SMEM),
            pl.BlockSpec((rows, length), lambda d: (0, 0)),
            pl.BlockSpec((length, 1), lambda d: (0, 0)),
            pl.BlockSpec((length, 1), lambda d: (0, 0)),
        ],
        out_specs=[pl.BlockSpec((1, rows // chunks, 4 * seg_width), lambda d: (d, 0, 0))] * chunks,
        out_shape=[
            jax.ShapeDtypeStruct((dests, rows // chunks, 4 * seg_width), jnp.bfloat16)
        ]
        * chunks,
        compiler_params=params(),
        cost_estimate=pl.CostEstimate(
            flops=2 * rows * length * 4 * seg_width * dests,
            bytes_accessed=2 * rows * (length + dests * 4 * seg_width),
            transcendentals=0,
        ),
    )(segs, tile, col_a, col_b)


def permute_kernel(sign_ref, block_ref, col_ref, out_ref):
    step = out_ref.shape[1]
    length = block_ref.shape[1]
    lane = lax.broadcasted_iota(jnp.int32, (length, step), 1) + pl.program_id(0) * step
    hot = (col_ref[...] == lane).astype(jnp.float32).astype(jnp.bfloat16)
    moved = jnp.dot(block_ref[...], hot, preferred_element_type=jnp.float32)
    out_ref[...] = (moved * sign_ref[0]).astype(jnp.bfloat16)


def permute_block(block, col, sign):
    rows, length = block.shape
    step = column_step(length)
    return pl.pallas_call(
        permute_kernel,
        grid=(length // step,),
        in_specs=[
            pl.BlockSpec(memory_space=SMEM),
            pl.BlockSpec((rows, length), lambda j: (0, 0)),
            pl.BlockSpec((length, 1), lambda j: (0, 0)),
        ],
        out_specs=pl.BlockSpec((rows, step), lambda j: (0, j)),
        out_shape=jax.ShapeDtypeStruct((rows, length), jnp.bfloat16),
        compiler_params=params(),
        cost_estimate=pl.CostEstimate(
            flops=2 * rows * length * length, bytes_accessed=4 * rows * length, transcendentals=0
        ),
    )(sign, block, col)


def energy_kernel(table_ref, index_ref, out_ref):
    count = table_ref.shape[1]
    step = out_ref.shape[1]
    value = table_ref[...]
    high = value.astype(jnp.bfloat16)
    rest = value - high.astype(jnp.float32)
    middle = rest.astype(jnp.bfloat16)
    low = (rest - middle.astype(jnp.float32)).astype(jnp.bfloat16)
    spot = lax.broadcasted_iota(jnp.int32, (count, step), 0)
    for row in range(2):
        hot = (spot == index_ref[row : row + 1, :]).astype(jnp.float32).astype(jnp.bfloat16)
        parts = [
            jnp.dot(piece, hot, preferred_element_type=jnp.float32)
            for piece in (high, middle, low)
        ]
        out_ref[row : row + 1, :] = (parts[0][0:1] + parts[1][0:1]) + parts[2][0:1]


def pair_energies(vir_energy, index):
    count = vir_energy.shape[0]
    length = index.shape[1]
    step = column_step(length)
    table = jnp.broadcast_to(vir_energy[None, :], (8, count))
    return pl.pallas_call(
        energy_kernel,
        grid=(length // step,),
        in_specs=[
            pl.BlockSpec((8, count), lambda j: (0, 0)),
            pl.BlockSpec((2, step), lambda j: (0, j)),
        ],
        out_specs=pl.BlockSpec((2, step), lambda j: (0, j)),
        out_shape=jax.ShapeDtypeStruct((2, length), jnp.float32),
        compiler_params=params(),
        cost_estimate=pl.CostEstimate(
            flops=2 * 256 * count * length * 2, bytes_accessed=4 * count * 8, transcendentals=0
        ),
    )(table, index)


def assemble_kernel(source_ref, sub_ref, in_ref, out_ref):
    out_ref[...] = in_ref[0]


def assemble(messages, source, sub, seg_width):
    rows = messages.shape[1]
    slots = source.shape[0]
    return pl.pallas_call(
        assemble_kernel,
        grid_spec=pltpu.PrefetchScalarGridSpec(
            num_scalar_prefetch=2,
            grid=(slots,),
            in_specs=[
                pl.BlockSpec((1, rows, seg_width), lambda j, src, sub: (src[j], 0, sub[j]))
            ],
            out_specs=pl.BlockSpec((rows, seg_width), lambda j, src, sub: (0, j)),
        ),
        out_shape=jax.ShapeDtypeStruct((rows, slots * seg_width), jnp.bfloat16),
        compiler_params=params(),
        cost_estimate=pl.CostEstimate(
            flops=0, bytes_accessed=4 * rows * slots * seg_width, transcendentals=0
        ),
    )(source, sub, messages)


def final_kernel(
    pieces, flag_ref, mine_ref, recv_ref, tile_ref, pair_ref, vir_ref, *rest
):
    blocks = rest[: 2 * pieces]
    out_ref, own_ref, other_ref = rest[-3:]
    width = own_ref.shape[1]

    @pl.when(pl.program_id(0) == 0)
    def _():
        upper = flag_ref[0] > 0
        mine_a = mine_ref[:, :width].astype(jnp.float32)
        recv_a = recv_ref[:, :width].astype(jnp.float32)
        mine_b = mine_ref[:, width:].astype(jnp.float32)
        recv_b = recv_ref[:, width:].astype(jnp.float32)
        sym = ((mine_a + recv_a) * 0.5).astype(jnp.bfloat16)
        sign = jnp.where(upper, 0.5, -0.5).astype(jnp.float32)
        anti = ((mine_b - recv_b) * sign).astype(jnp.bfloat16)

        @pl.when(upper)
        def _():
            own_ref[...] = anti
            other_ref[...] = sym

        @pl.when(jnp.logical_not(upper))
        def _():
            own_ref[...] = sym
            other_ref[...] = anti

    depth = blocks[0].shape[0]
    step = column_step(out_ref.shape[1])
    for start in range(0, out_ref.shape[1], step):
        at_columns = slice(start, start + step)
        total = None
        for held, part in ((own_ref, blocks[:pieces]), (other_ref, blocks[pieces:])):
            for at, block in enumerate(part):
                term = jnp.dot(
                    held[:, at * depth : (at + 1) * depth],
                    block[:, at_columns],
                    preferred_element_type=jnp.float32,
                )
                total = term if total is None else total + term
        denominator = pair_ref[...] - vir_ref[0:1, at_columns] - vir_ref[1:2, at_columns]
        raw = tile_ref[:, at_columns].astype(jnp.float32)
        out_ref[:, at_columns] = (raw + total / denominator).astype(jnp.bfloat16)


def finish(at, earlier, flag, mine, recv, tile, pair_energy, energies, own_blocks, mirror_blocks):
    length = tile.shape[1]
    rows = mine.shape[0]
    width = mine.shape[1] // 2
    pieces = len(own_blocks)
    depth = own_blocks[0].shape[0]
    small = 4 * pieces * depth * length <= 8 << 20
    step = length if small else column_step(length) // 2
    before = [] if earlier is None else [earlier]
    whole = lambda j: (0, 0)
    across = lambda j: (0, j)
    return pl.pallas_call(
        functools.partial(final_kernel, pieces),
        grid=(length // step,),
        in_specs=[
            pl.BlockSpec(memory_space=SMEM),
            pl.BlockSpec(mine.shape, whole),
            pl.BlockSpec(recv.shape, whole),
            pl.BlockSpec((rows, step), lambda j: (at, j)),
            pl.BlockSpec((rows, 1), lambda j: (at, 0)),
            pl.BlockSpec((2, step), across),
        ]
        + [pl.BlockSpec((depth, step), across)] * (2 * pieces)
        + [pl.BlockSpec(memory_space=pl.ANY)] * len(before),
        out_specs=pl.BlockSpec((rows, step), lambda j: (at, j)),
        out_shape=jax.ShapeDtypeStruct(tile.shape, jnp.bfloat16),
        input_output_aliases={6 + 2 * pieces: 0} if before else {},
        scratch_shapes=[VMEM((rows, width), jnp.bfloat16)] * 2,
        compiler_params=params(56 << 20),
        cost_estimate=pl.CostEstimate(
            flops=4 * rows * width * length,
            bytes_accessed=4 * (rows * length + width * length),
            transcendentals=0,
        ),
    )(flag, mine, recv, tile, pair_energy[:, None], energies, *own_blocks, *mirror_blocks, *before)


def gather_pieces(block):
    pieces = [block]
    bit = lax.axis_size("pair") // 2
    order = [0]
    while bit:
        pieces += [swap(piece, "pair", bit) for piece in pieces]
        order += [at ^ bit for at in order]
        bit //= 2
    return pieces, order


def local(
    amplitudes, integrals, screen_list, block_owner, mirror_map, pair_virt, vir_energy, pair_energy
):
    owners = lax.axis_size(OWNERS)
    half = owners // 2
    self_index = lax.axis_index(OWNERS)
    upper = self_index >= half
    folded = self_index % half
    tile = amplitudes[:, 0, :]
    rows, length = tile.shape
    per, seg_width = integrals.shape[1:3]
    count = block_owner.shape[1]

    row = jnp.concatenate(
        [block_owner, screen_list, upper.astype(jnp.int32).reshape(1, 1), folded.reshape(1, 1)],
        axis=1,
    )
    row = jnp.pad(row, ((0, 7), (0, -row.shape[1] % 128)))
    table = exchange_tables(row)

    map_col = lax.dynamic_index_in_dim(mirror_map, self_index, 0, keepdims=False)[:, None]
    straight = lax.broadcasted_iota(jnp.int32, (length, 1), 0)
    col_a = jnp.where(upper, map_col, straight)
    col_b = jnp.where(upper, straight, map_col)
    shard = integrals[0].reshape(per * seg_width, length)
    sign = jnp.where(upper, 1.0, -1.0).astype(jnp.float32)[None]
    own_blocks, order = gather_pieces(shard)
    back_col = lax.dynamic_index_in_dim(
        mirror_map, (self_index + half) % owners, 0, keepdims=False
    )[:, None]
    mirror_shard = permute_block(swap(shard, OWNERS, half), back_col, sign)
    mirror_blocks, _ = gather_pieces(mirror_shard)

    chunks = chunk_count(rows, half)
    outgoing = select_segments(tile, col_a, col_b, table, count, seg_width, chunks)
    pair_at = lax.axis_index("pair")
    slot = (
        jnp.concatenate([(pair_at ^ at) * per + jnp.arange(per, dtype=jnp.int32) for at in order])
    )
    slot_hot = slot[:, None] == jnp.arange(count, dtype=jnp.int32)[None, :]
    own_row, other_row = table[0, :count], table[half, :count]
    dest_owner = jnp.stack(
        [jnp.where(upper, other_row, own_row), jnp.where(upper, own_row, other_row)]
    )
    mine_owner = jnp.sum(jnp.where(slot_hot[None], dest_owner[:, None, :], 0), axis=2)
    source = ((mine_owner % half) ^ folded).reshape(-1)
    sub = (mine_owner // half + jnp.array([[0], [2]], jnp.int32)).reshape(-1)
    energies = pair_energies(vir_energy, pair_virt[0])
    flag = upper.astype(jnp.int32)[None]
    updated = None
    for at in range(chunks):
        messages = [outgoing[at][0]] + [
            swap(outgoing[at][d], OWNERS, d) for d in range(1, half)
        ]
        mine = assemble(jnp.stack(messages), source, sub, seg_width)
        recv = swap(mine, OWNERS, half)
        updated = finish(
            at, updated, flag, mine, recv, tile, pair_energy, energies, own_blocks, mirror_blocks
        )
    return updated[:, None, :]


def solution(mesh):
    placed = (
        P("pair", OWNERS, None),
        P(OWNERS, "pair", None, None),
        P(OWNERS, None),
        P(OWNERS, None),
        P(),
        P(OWNERS, None, None),
        P(),
        P("pair"),
    )
    return jax.shard_map(
        local,
        mesh=mesh,
        in_specs=placed,
        out_specs=P("pair", OWNERS, None),
        check_vma=False,
    )
```

```python
import functools

import jax
import jax.numpy as jnp
from jax import lax
from jax.experimental import pallas as pl
from jax.experimental.pallas import tpu as pltpu
from jax.sharding import PartitionSpec as P

OWNERS = ("bra", "ket")
CHUNKS = 2
VMEM = pltpu.VMEM
SMEM = pltpu.SMEM


def swap(block, axis, bit):
    count = lax.axis_size(axis)
    return lax.ppermute(block, axis, [(i, i ^ bit) for i in range(count)])


def column_step(length):
    return next(step for step in (512, 256, 128, length) if length % step == 0)


def params(limit=48 << 20):
    return pltpu.CompilerParams(vmem_limit_bytes=limit)


def chunk_count(rows, half):
    if half > 8:
        return 1
    return next(c for c in (CHUNKS, 3, 2, 1) if c == 1 or rows % (16 * c) == 0)


def table_kernel(owners, ket, row_ref, out_ref, held, send_sem, recv_sem):
    me = lax.axis_index(OWNERS)
    peers = [me ^ d for d in range(owners)]
    places = [{"bra": peer // ket, "ket": peer % ket} for peer in peers]
    barrier = pltpu.get_barrier_semaphore()
    for d in range(1, owners):
        pl.semaphore_signal(
            barrier, inc=1, device_id=places[d], device_id_type=pl.DeviceIdType.MESH
        )
    pl.semaphore_wait(barrier, owners - 1)
    copies = []
    for d in range(1, owners):
        copy = pltpu.make_async_remote_copy(
            src_ref=row_ref,
            dst_ref=held.at[d],
            send_sem=send_sem.at[d],
            recv_sem=recv_sem.at[d],
            device_id=places[d],
            device_id_type=pl.DeviceIdType.MESH,
        )
        copy.start()
        copies.append(copy)
    out_ref[0:1, :] = row_ref[0:1, :]
    for d in range(1, owners):
        copies[d - 1].wait()
        out_ref[d : d + 1, :] = held[d, 0:1, :]


def exchange_tables(row):
    owners = lax.axis_size(OWNERS)
    width = row.shape[1]
    return pl.pallas_call(
        functools.partial(table_kernel, owners, lax.axis_size("ket")),
        in_specs=[pl.BlockSpec(memory_space=VMEM)],
        out_specs=pl.BlockSpec(memory_space=VMEM),
        out_shape=jax.ShapeDtypeStruct((owners, width), jnp.int32),
        scratch_shapes=[
            VMEM((owners, 8, width), jnp.int32),
            pltpu.SemaphoreType.DMA((owners,)),
            pltpu.SemaphoreType.DMA((owners,)),
        ],
        compiler_params=pltpu.CompilerParams(
            collective_id=1, has_side_effects=True, vmem_limit_bytes=8 << 20
        ),
    )(row)


def select_kernel(count, seg_width, segs_ref, tile_ref, col_a_ref, col_b_ref, *out_refs):
    dest = pl.program_id(0)
    half = pl.num_programs(0)
    flip = segs_ref[0, 2 * count] * half
    folded = segs_ref[0, 2 * count + 1]
    length = tile_ref.shape[1]
    lane = lax.broadcasted_iota(jnp.int32, (length, seg_width), 1)
    hots = []
    for sub in range(4):
        col = (col_a_ref, col_b_ref)[sub // 2]
        row = dest + (flip if sub < 2 else half - flip)
        serving = folded + (sub % 2) * half
        segment = jnp.int32(0)
        for k in range(count):
            held = segs_ref[row, k] == serving
            segment += jnp.where(held, segs_ref[row, count + k], 0)
        base = segment * seg_width
        hots.append((col[...] == lane + base).astype(jnp.float32).astype(jnp.bfloat16))
    hot = jnp.concatenate(hots, axis=1)
    part = out_refs[0].shape[1]
    for at, out_ref in enumerate(out_refs):
        out_ref[0] = jnp.dot(
            tile_ref[at * part : (at + 1) * part, :], hot, preferred_element_type=jnp.float32
        ).astype(jnp.bfloat16)


def select_segments(tile, col_a, col_b, segs, count, seg_width, chunks):
    rows, length = tile.shape
    dests = segs.shape[0] // 2
    return pl.pallas_call(
        functools.partial(select_kernel, count, seg_width),
        grid=(dests,),
        in_specs=[
            pl.BlockSpec(memory_space=SMEM),
            pl.BlockSpec((rows, length), lambda d: (0, 0)),
            pl.BlockSpec((length, 1), lambda d: (0, 0)),
            pl.BlockSpec((length, 1), lambda d: (0, 0)),
        ],
        out_specs=[pl.BlockSpec((1, rows // chunks, 4 * seg_width), lambda d: (d, 0, 0))] * chunks,
        out_shape=[
            jax.ShapeDtypeStruct((dests, rows // chunks, 4 * seg_width), jnp.bfloat16)
        ]
        * chunks,
        compiler_params=params(),
        cost_estimate=pl.CostEstimate(
            flops=2 * rows * length * 4 * seg_width * dests,
            bytes_accessed=2 * rows * (length + dests * 4 * seg_width),
            transcendentals=0,
        ),
    )(segs, tile, col_a, col_b)


def permute_kernel(sign_ref, block_ref, col_ref, out_ref):
    step = out_ref.shape[1]
    length = block_ref.shape[1]
    lane = lax.broadcasted_iota(jnp.int32, (length, step), 1) + pl.program_id(0) * step
    hot = (col_ref[...] == lane).astype(jnp.float32).astype(jnp.bfloat16)
    moved = jnp.dot(block_ref[...], hot, preferred_element_type=jnp.float32)
    out_ref[...] = (moved * sign_ref[0]).astype(jnp.bfloat16)


def permute_block(block, col, sign):
    rows, length = block.shape
    step = column_step(length)
    return pl.pallas_call(
        permute_kernel,
        grid=(length // step,),
        in_specs=[
            pl.BlockSpec(memory_space=SMEM),
            pl.BlockSpec((rows, length), lambda j: (0, 0)),
            pl.BlockSpec((length, 1), lambda j: (0, 0)),
        ],
        out_specs=pl.BlockSpec((rows, step), lambda j: (0, j)),
        out_shape=jax.ShapeDtypeStruct((rows, length), jnp.bfloat16),
        compiler_params=params(),
        cost_estimate=pl.CostEstimate(
            flops=2 * rows * length * length, bytes_accessed=4 * rows * length, transcendentals=0
        ),
    )(sign, block, col)


def energy_kernel(table_ref, index_ref, out_ref):
    count = table_ref.shape[1]
    step = out_ref.shape[1]
    value = table_ref[...]
    high = value.astype(jnp.bfloat16)
    rest = value - high.astype(jnp.float32)
    middle = rest.astype(jnp.bfloat16)
    low = (rest - middle.astype(jnp.float32)).astype(jnp.bfloat16)
    spot = lax.broadcasted_iota(jnp.int32, (count, step), 0)
    for row in range(2):
        hot = (spot == index_ref[row : row + 1, :]).astype(jnp.float32).astype(jnp.bfloat16)
        parts = [
            jnp.dot(piece, hot, preferred_element_type=jnp.float32)
            for piece in (high, middle, low)
        ]
        out_ref[row : row + 1, :] = (parts[0][0:1] + parts[1][0:1]) + parts[2][0:1]


def pair_energies(vir_energy, index):
    count = vir_energy.shape[0]
    length = index.shape[1]
    step = column_step(length)
    table = jnp.broadcast_to(vir_energy[None, :], (8, count))
    return pl.pallas_call(
        energy_kernel,
        grid=(length // step,),
        in_specs=[
            pl.BlockSpec((8, count), lambda j: (0, 0)),
            pl.BlockSpec((2, step), lambda j: (0, j)),
        ],
        out_specs=pl.BlockSpec((2, step), lambda j: (0, j)),
        out_shape=jax.ShapeDtypeStruct((2, length), jnp.float32),
        compiler_params=params(),
        cost_estimate=pl.CostEstimate(
            flops=2 * 256 * count * length * 2, bytes_accessed=4 * count * 8, transcendentals=0
        ),
    )(table, index)


def assemble_kernel(source_ref, sub_ref, in_ref, out_ref):
    out_ref[...] = in_ref[0]


def pick_kernel(seg_width, source_ref, sub_ref, *refs):
    out_ref = refs[-1]
    for slot in range(out_ref.shape[1] // seg_width):
        columns = pl.ds(pl.multiple_of(sub_ref[slot] * seg_width, seg_width), seg_width)
        for at, message in enumerate(refs[:-1]):

            @pl.when(source_ref[slot] == at)
            def _():
                out_ref[:, slot * seg_width : (slot + 1) * seg_width] = message[:, columns]


def assemble(messages, source, sub, seg_width):
    if len(messages) <= 8 and seg_width % 128 == 0:
        rows = messages[0].shape[0]
        return pl.pallas_call(
            functools.partial(pick_kernel, seg_width),
            in_specs=[pl.BlockSpec(memory_space=SMEM)] * 2
            + [pl.BlockSpec(memory_space=VMEM)] * len(messages),
            out_specs=pl.BlockSpec(memory_space=VMEM),
            out_shape=jax.ShapeDtypeStruct((rows, source.shape[0] * seg_width), jnp.bfloat16),
            compiler_params=params(16 << 20),
        )(source, sub, *messages)
    messages = jnp.stack(messages)
    rows = messages.shape[1]
    slots = source.shape[0]
    return pl.pallas_call(
        assemble_kernel,
        grid_spec=pltpu.PrefetchScalarGridSpec(
            num_scalar_prefetch=2,
            grid=(slots,),
            in_specs=[
                pl.BlockSpec((1, rows, seg_width), lambda j, src, sub: (src[j], 0, sub[j]))
            ],
            out_specs=pl.BlockSpec((rows, seg_width), lambda j, src, sub: (0, j)),
        ),
        out_shape=jax.ShapeDtypeStruct((rows, slots * seg_width), jnp.bfloat16),
        compiler_params=params(),
        cost_estimate=pl.CostEstimate(
            flops=0, bytes_accessed=4 * rows * slots * seg_width, transcendentals=0
        ),
    )(source, sub, messages)


def final_kernel(
    pieces, flag_ref, mine_ref, recv_ref, tile_ref, pair_ref, vir_ref, *rest
):
    blocks = rest[: 2 * pieces]
    out_ref, own_ref, other_ref = rest[-3:]
    width = own_ref.shape[1]

    @pl.when(pl.program_id(0) == 0)
    def _():
        upper = flag_ref[0] > 0
        mine_a = mine_ref[:, :width].astype(jnp.float32)
        recv_a = recv_ref[:, :width].astype(jnp.float32)
        mine_b = mine_ref[:, width:].astype(jnp.float32)
        recv_b = recv_ref[:, width:].astype(jnp.float32)
        sym = ((mine_a + recv_a) * 0.5).astype(jnp.bfloat16)
        sign = jnp.where(upper, 0.5, -0.5).astype(jnp.float32)
        anti = ((mine_b - recv_b) * sign).astype(jnp.bfloat16)

        @pl.when(upper)
        def _():
            own_ref[...] = anti
            other_ref[...] = sym

        @pl.when(jnp.logical_not(upper))
        def _():
            own_ref[...] = sym
            other_ref[...] = anti

    depth = blocks[0].shape[0]
    step = column_step(out_ref.shape[1])
    for start in range(0, out_ref.shape[1], step):
        at_columns = slice(start, start + step)
        total = None
        for held, part in ((own_ref, blocks[:pieces]), (other_ref, blocks[pieces:])):
            for at, block in enumerate(part):
                term = jnp.dot(
                    held[:, at * depth : (at + 1) * depth],
                    block[:, at_columns],
                    preferred_element_type=jnp.float32,
                )
                total = term if total is None else total + term
        denominator = pair_ref[...] - vir_ref[0:1, at_columns] - vir_ref[1:2, at_columns]
        raw = tile_ref[:, at_columns].astype(jnp.float32)
        out_ref[:, at_columns] = (raw + total / denominator).astype(jnp.bfloat16)


def finish(at, earlier, flag, mine, recv, tile, pair_energy, energies, own_blocks, mirror_blocks):
    length = tile.shape[1]
    rows = mine.shape[0]
    width = mine.shape[1] // 2
    pieces = len(own_blocks)
    depth = own_blocks[0].shape[0]
    small = 4 * pieces * depth * length <= 8 << 20
    step = length if small else column_step(length) // 2
    before = [] if earlier is None else [earlier]
    whole = lambda j: (0, 0)
    across = lambda j: (0, j)
    return pl.pallas_call(
        functools.partial(final_kernel, pieces),
        grid=(length // step,),
        in_specs=[
            pl.BlockSpec(memory_space=SMEM),
            pl.BlockSpec(mine.shape, whole),
            pl.BlockSpec(recv.shape, whole),
            pl.BlockSpec((rows, step), lambda j: (at, j)),
            pl.BlockSpec((rows, 1), lambda j: (at, 0)),
            pl.BlockSpec((2, step), across),
        ]
        + [pl.BlockSpec((depth, step), across)] * (2 * pieces)
        + [pl.BlockSpec(memory_space=pl.ANY)] * len(before),
        out_specs=pl.BlockSpec((rows, step), lambda j: (at, j)),
        out_shape=jax.ShapeDtypeStruct(tile.shape, jnp.bfloat16),
        input_output_aliases={6 + 2 * pieces: 0} if before else {},
        scratch_shapes=[VMEM((rows, width), jnp.bfloat16)] * 2,
        compiler_params=params(56 << 20),
        cost_estimate=pl.CostEstimate(
            flops=4 * rows * width * length,
            bytes_accessed=4 * (rows * length + width * length),
            transcendentals=0,
        ),
    )(flag, mine, recv, tile, pair_energy[:, None], energies, *own_blocks, *mirror_blocks, *before)


def gather_pieces(block):
    pieces = [block]
    bit = lax.axis_size("pair") // 2
    order = [0]
    while bit:
        pieces += [swap(piece, "pair", bit) for piece in pieces]
        order += [at ^ bit for at in order]
        bit //= 2
    return pieces, order


def local(
    amplitudes, integrals, screen_list, block_owner, mirror_map, pair_virt, vir_energy, pair_energy
):
    owners = lax.axis_size(OWNERS)
    half = owners // 2
    self_index = lax.axis_index(OWNERS)
    upper = self_index >= half
    folded = self_index % half
    tile = amplitudes[:, 0, :]
    rows, length = tile.shape
    per, seg_width = integrals.shape[1:3]
    count = block_owner.shape[1]

    row = jnp.concatenate(
        [block_owner, screen_list, upper.astype(jnp.int32).reshape(1, 1), folded.reshape(1, 1)],
        axis=1,
    )
    row = jnp.pad(row, ((0, 7), (0, -row.shape[1] % 128)))
    table = exchange_tables(row)

    map_col = lax.dynamic_index_in_dim(mirror_map, self_index, 0, keepdims=False)[:, None]
    straight = lax.broadcasted_iota(jnp.int32, (length, 1), 0)
    col_a = jnp.where(upper, map_col, straight)
    col_b = jnp.where(upper, straight, map_col)
    shard = integrals[0].reshape(per * seg_width, length)
    sign = jnp.where(upper, 1.0, -1.0).astype(jnp.float32)[None]
    shard, table = lax.optimization_barrier((shard, table))
    own_blocks, order = gather_pieces(shard)
    back_col = lax.dynamic_index_in_dim(
        mirror_map, (self_index + half) % owners, 0, keepdims=False
    )[:, None]
    mirror_shard = permute_block(swap(shard, OWNERS, half), back_col, sign)
    mirror_blocks, _ = gather_pieces(mirror_shard)

    chunks = chunk_count(rows, half)
    outgoing = select_segments(tile, col_a, col_b, table, count, seg_width, chunks)
    pair_at = lax.axis_index("pair")
    slot = (
        jnp.concatenate([(pair_at ^ at) * per + jnp.arange(per, dtype=jnp.int32) for at in order])
    )
    slot_hot = slot[:, None] == jnp.arange(count, dtype=jnp.int32)[None, :]
    own_row, other_row = table[0, :count], table[half, :count]
    dest_owner = jnp.stack(
        [jnp.where(upper, other_row, own_row), jnp.where(upper, own_row, other_row)]
    )
    mine_owner = jnp.sum(jnp.where(slot_hot[None], dest_owner[:, None, :], 0), axis=2)
    source = ((mine_owner % half) ^ folded).reshape(-1)
    sub = (mine_owner // half + jnp.array([[0], [2]], jnp.int32)).reshape(-1)
    energies = pair_energies(vir_energy, pair_virt[0])
    flag = upper.astype(jnp.int32)[None]
    updated = None
    for at in range(chunks):
        messages = [outgoing[at][0]] + [
            swap(outgoing[at][d], OWNERS, d) for d in range(1, half)
        ]
        mine = assemble(messages, source, sub, seg_width)
        recv = swap(mine, OWNERS, half)
        updated = finish(
            at, updated, flag, mine, recv, tile, pair_energy, energies, own_blocks, mirror_blocks
        )
    return updated[:, None, :]


def solution(mesh):
    placed = (
        P("pair", OWNERS, None),
        P(OWNERS, "pair", None, None),
        P(OWNERS, None),
        P(OWNERS, None),
        P(),
        P(OWNERS, None, None),
        P(),
        P("pair"),
    )
    return jax.shard_map(
        local,
        mesh=mesh,
        in_specs=placed,
        out_specs=P("pair", OWNERS, None),
        check_vma=False,
    )
```
